32 devices in a mesh: slab: 2 (over x), row: 8 (over z, y), col: 2 (over core).
Axes of the slice: x: 2, y: 2, z: 4, core: 2. Of those that a mesh axis runs over, the one named last changes fastest.
Arguments:
- points: bfloat16 [9, 32, 131072], P(None, None, ('slab', 'row', 'col')), parts along dimension 2, may hold values from -6 to 6
- pillar_cell: int32 [131072], P(('slab', 'row', 'col')), parts along dimension 0, may hold values from 0 to 65535, as said below
- point_count: int32 [131072], P(('slab', 'row', 'col')), parts along dimension 0, may hold values from 1 to 32
- tile_count: int32 [512], P(('slab', 'row', 'col')), parts along dimension 0, may hold values from 0 to 256, as said below
- point_embed: bfloat16 [64, 9], replicated, may hold values from -3 to 3
- point_mix: bfloat16 [64, 64], replicated, may hold values from -1 to 1
- first_conv: bfloat16 [3, 3, 64, 64], replicated, may hold values from -0.375 to 0.375
- second_conv: bfloat16 [3, 3, 64, 64], replicated, may hold values from -0.375 to 0.375
- third_conv: bfloat16 [3, 3, 128, 64], replicated, may hold values from -0.375 to 0.375
- fourth_conv: bfloat16 [3, 3, 128, 128], replicated, may hold values from -0.25 to 0.25
- fifth_conv: bfloat16 [3, 3, 256, 128], replicated, may hold values from -0.25 to 0.25
- sixth_conv: bfloat16 [3, 3, 256, 256], replicated, may hold values from -0.1875 to 0.1875
- near_lift: bfloat16 [1, 1, 128, 64], replicated, may hold values from -1 to 1
- mid_lift: bfloat16 [2, 2, 128, 128], replicated, may hold values from -0.75 to 0.75
- far_lift: bfloat16 [4, 4, 128, 256], replicated, may hold values from -0.5 to 0.5
- biases: float32 [1408], replicated, may hold values from -1.5 to 1.5
Outputs:
- joined: bfloat16 [384, 256, 512], P(None, ('slab', 'row'), 'col'), parts along dimension 1
The draws below stay inside these ranges and needn't reach their ends.
There are 2 independent parts, one for each index of `slab`. The reference program is written for one: setup_inputs(seed, part) draws one part's arguments, and reference() takes and returns one part's arrays. A program takes and returns all parts, laid end to end along the dimension named above; an argument that names none is the same for every part. Nothing has to cross between parts.
Inputs may be any that keep to these rules, and one draw needn't show every extreme that they name: `tile_count`: entry s * 16 + t counts the live slots that device s (row-major over row and col) holds for tile t (row-major over row and col); they are the first of that tile's group of 256 slots. In every draw some tile gets exactly 256 live slots from every device. `pillar_cell`: slot s holds cell r * 512 + c; every slot in a device's group for tile t lies in tile t, whose rows and columns are those of device t; a cell may appear in several slots, on one device or several. `point_count`: the valid points of a slot are its first ones.
All inputs are finite; a program needn't handle non-finite values.
Results may differ from the reference program's by a relative error of at most 0.0081.
Values may be sent and summed in bfloat16 or wider, within the bound.
A program may use at most 64 MiB of HBM per device.

```python
import jax
import jax.numpy as jnp
from jax import lax

FEAT = 9
PTS = 32
PF = 64
C1 = 64
C2 = 128
C3 = 256
UP = 128
ROWS_DEV = 16
COLS_DEV = 256
CAP = 256
TILES = 16
ALLSLOTS = 65536
NROWS = 128
NCOLS = 512
BIAS_LEN = 1408


def draw_pillar_cell(key, part):
    col_tiles = NCOLS // COLS_DEV
    slot_index = jnp.arange(ALLSLOTS, dtype=jnp.int32)
    dest_tile = slot_index // CAP % TILES
    tile_row = dest_tile // col_tiles
    tile_col = dest_tile % col_tiles
    key_row, key_col = jax.random.split(jax.random.fold_in(key, 11))
    row_inside = jax.random.randint(key_row, (ALLSLOTS,), 0, ROWS_DEV, dtype=jnp.int32)
    col_inside = jax.random.randint(key_col, (ALLSLOTS,), 0, COLS_DEV, dtype=jnp.int32)
    return ((tile_row * ROWS_DEV + row_inside) * NCOLS + tile_col * COLS_DEV + col_inside).astype(jnp.int32)


def draw_tile_count(key, part):
    key_hot, key_load = jax.random.split(jax.random.fold_in(key, 23))
    hottest = jax.random.randint(key_hot, (), 0, TILES, dtype=jnp.int32)
    load_draw = jax.random.randint(key_load, (TILES, TILES), 0, CAP * 4 // 5 + 1, dtype=jnp.int32)
    dest_tile = lax.broadcasted_iota(jnp.int32, (TILES, TILES), 1)
    return jnp.where(dest_tile == hottest, CAP, load_draw).reshape(TILES * TILES).astype(jnp.int32)


def with_ends(values, rng, smallest, top_value):
    place = [jax.random.randint(jax.random.fold_in(rng, axis), (), 0, length) for axis, length in enumerate(values.shape)]
    widest = values.shape.index(max(values.shape))
    neighbour = place[:widest] + [(place[widest] + 1) % values.shape[widest]] + place[widest + 1:]
    return values.at[tuple(place)].set(smallest).at[tuple(neighbour)].set(top_value)


def steps_of(stream_key, dims, cuts, least, largest):
    loudness, own = 1.0, jax.random.fold_in(stream_key, 6)
    for axis_at, blocks in cuts:
        steps = jnp.exp(jax.random.uniform(jax.random.fold_in(own, axis_at), (blocks,), jnp.float32, least / len(cuts), largest / len(cuts)))
        loudness = loudness * jnp.repeat(steps, dims[axis_at] // blocks).reshape([-1 if axis == axis_at else 1 for axis in range(len(dims))])
    return loudness


def bell_draw(rng, shape, spread, most, shards=(), kind=jnp.bfloat16):
    drawn = spread * jax.random.normal(rng, shape, jnp.float32)
    if shards:
        drawn = drawn * steps_of(rng, shape, shards, -0.22, 0.18)
    return jnp.clip(drawn, -most, most).astype(kind)


def setup_inputs(seed: int = 0, part: int = 0) -> dict:
    keys = jax.random.split(jax.random.key(seed), 17)
    part_splits = jax.random.split(jax.random.fold_in(keys[16], part), 17)
    return {
        "points": bell_draw(part_splits[0], (FEAT, PTS, ALLSLOTS), 1.0, 6.0, ((2, 16),)),
        "pillar_cell": draw_pillar_cell(jax.random.fold_in(jax.random.fold_in(keys[16], part), 71), part),
        "point_count": with_ends(jax.random.randint(part_splits[2], (ALLSLOTS,), 1, PTS + 1), jax.random.fold_in(part_splits[2], 1), 1, PTS).astype(jnp.int32),
        "tile_count": draw_tile_count(jax.random.fold_in(jax.random.fold_in(keys[16], part), 71), part),
        "point_embed": bell_draw(keys[4], (PF, FEAT), (FEAT // 2) ** -0.5, 3.0),
        "point_mix": bell_draw(keys[5], (PF, PF), (PF // 2) ** -0.5, 1.0),
        "first_conv": bell_draw(keys[6], (3, 3, C1, PF), (9 * PF // 2) ** -0.5, 0.375),
        "second_conv": bell_draw(keys[7], (3, 3, C1, C1), (9 * C1 // 2) ** -0.5, 0.375),
        "third_conv": bell_draw(keys[8], (3, 3, C2, C1), (9 * C1 // 2) ** -0.5, 0.375),
        "fourth_conv": bell_draw(keys[9], (3, 3, C2, C2), (9 * C2 // 2) ** -0.5, 0.25),
        "fifth_conv": bell_draw(keys[10], (3, 3, C3, C2), (9 * C2 // 2) ** -0.5, 0.25),
        "sixth_conv": bell_draw(keys[11], (3, 3, C3, C3), (9 * C3 // 2) ** -0.5, 0.1875),
        "near_lift": bell_draw(keys[12], (1, 1, UP, C1), (C1 // 2) ** -0.5, 1.0),
        "mid_lift": bell_draw(keys[13], (2, 2, UP, C2), (C2 // 2) ** -0.5, 0.75),
        "far_lift": bell_draw(keys[14], (4, 4, UP, C3), (C3 // 2) ** -0.5, 0.5),
        "biases": bell_draw(keys[15], (BIAS_LEN,), 0.3, 1.5, (), jnp.float32),
    }


def encode_block(point_block, count_row, point_embed, point_mix, b_embed, b_mix):
    feat_in, point_num, slot_num = point_block.shape
    flat_rows = point_block.reshape(feat_in, point_num * slot_num)
    hidden = jnp.dot(point_embed, flat_rows, preferred_element_type=jnp.float32) + b_embed[:, None]
    hidden = jax.nn.relu(hidden).astype(jnp.bfloat16)
    second = jnp.dot(point_mix, hidden, preferred_element_type=jnp.float32) + b_mix[:, None]
    second = jax.nn.relu(second).reshape(-1, point_num, slot_num)
    valid_mask = lax.broadcasted_iota(jnp.int32, (point_num, slot_num), 0) < count_row[None, :]
    return jnp.max(jnp.where(valid_mask[None], second, 0.0), axis=1).astype(jnp.bfloat16)


def conv_layer(inputs, kernel, bias_vec, stride):
    summed = lax.conv_general_dilated(inputs[None], kernel, (stride, stride), ((1, 1), (1, 1)),
                                      dimension_numbers=("NCHW", "HWOI", "NCHW"),
                                      preferred_element_type=jnp.float32)[0]
    return jax.nn.relu(summed + bias_vec[:, None, None]).astype(jnp.bfloat16)


def lift_layer(inputs, kernel, bias_vec):
    factor = kernel.shape[0]
    product = jnp.einsum("abop,pij->oiajb", kernel.astype(jnp.float32), inputs.astype(jnp.float32))
    out_chan = kernel.shape[2]
    product = product.reshape(out_chan, inputs.shape[1] * factor, inputs.shape[2] * factor)
    return jax.nn.relu(product + bias_vec[:, None, None]).astype(jnp.bfloat16)


def reference(points, pillar_cell, point_count, tile_count, point_embed, point_mix, first_conv, second_conv,
              third_conv, fourth_conv, fifth_conv, sixth_conv, near_lift, mid_lift, far_lift, biases):
    extents = [PF, PF, C1, C1, C2, C2, C3, C3, UP, UP, UP]
    pieces = []
    offset = 0
    for extent in extents:
        pieces.append(biases[offset:offset + extent])
        offset += extent
    slot_index = jnp.arange(ALLSLOTS, dtype=jnp.int32)
    live_slot = (slot_index % CAP) < tile_count[slot_index // CAP]
    slot_points = jnp.where(live_slot, point_count, 0).astype(jnp.int32)

    def one_block(block_id):
        start = (block_id * CAP).astype(jnp.int32)
        point_block = lax.dynamic_slice_in_dim(points, start, CAP, 2)
        count_row = lax.dynamic_slice_in_dim(slot_points, start, CAP, 0)
        return encode_block(point_block, count_row, point_embed, point_mix, pieces[0], pieces[1])

    vectors = lax.map(one_block, jnp.arange(ALLSLOTS // CAP, dtype=jnp.int32))
    vectors = jnp.transpose(vectors, (1, 0, 2)).reshape(PF, ALLSLOTS)
    bev = jnp.zeros((PF, NROWS * NCOLS), jnp.bfloat16).at[:, pillar_cell].max(vectors)
    bev = bev.reshape(PF, NROWS, NCOLS)
    level_one = conv_layer(conv_layer(bev, first_conv, pieces[2], 1), second_conv, pieces[3], 1)
    level_two = conv_layer(conv_layer(level_one, third_conv, pieces[4], 2), fourth_conv, pieces[5], 1)
    level_three = conv_layer(conv_layer(level_two, fifth_conv, pieces[6], 2), sixth_conv, pieces[7], 1)
    near = lift_layer(level_one, near_lift, pieces[8])
    middle = lift_layer(level_two, mid_lift, pieces[9])
    distant = lift_layer(level_three, far_lift, pieces[10])
    return jnp.concatenate([near, middle, distant], axis=0)
```

```python
import functools

import jax
import jax.numpy as jnp
from jax import lax
from jax.experimental import pallas as pl
from jax.experimental.pallas import tpu as pltpu
from jax.sharding import PartitionSpec as P

ROWS_DEV = 16
COLS_DEV = 256
PACK = 4
HALF = 16
LANES = 4


def with_halo(block, sides, before, after):
    for axis, dim in sides:
        count = lax.axis_size(axis)
        forward = [(i, i + 1) for i in range(count - 1)]
        backward = [(target, source) for source, target in forward]
        size = block.shape[dim]
        low = lax.ppermute(lax.slice_in_dim(block, size - before, size, axis=dim), axis, forward)
        high = lax.ppermute(lax.slice_in_dim(block, 0, after, axis=dim), axis, backward)
        block = jnp.concatenate([low, block, high], axis=dim)
    return block


def encode_kernel(tiles, x_ref, meta_ref, w1_ref, w2_ref, b1_ref, b2_ref, out_ref):
    chan = b2_ref.shape[0]
    cap = meta_ref.shape[2]
    points = x_ref.shape[1]
    feat = x_ref.shape[0]
    for t in range(tiles):
        count = meta_ref[t, 0:1, :]
        best = jnp.full((chan, cap), -jnp.inf, jnp.float32)
        for h in range(points // HALF):
            block = x_ref[:, h * HALF : (h + 1) * HALF, t * cap : (t + 1) * cap]
            block = block.reshape(feat * HALF, cap)
            for q in range(HALF // PACK):
                hidden = jnp.dot(w1_ref[q], block, preferred_element_type=jnp.float32)
                hidden = jnp.maximum(hidden + b1_ref[...], 0.0).astype(jnp.bfloat16)
                second = jnp.dot(w2_ref[...], hidden, preferred_element_type=jnp.float32)
                for p in range(PACK):
                    j = h * HALF + q * PACK + p
                    part = second[p * chan : (p + 1) * chan]
                    best = jnp.maximum(best, jnp.where(count > j, part, -jnp.inf))
        vec = jnp.maximum(best + b2_ref[...], 0.0)
        out_ref[t, 0:chan, :] = vec.astype(jnp.bfloat16)
        which = lax.broadcasted_iota(jnp.int32, (16, cap), 0)
        row = jnp.broadcast_to(meta_ref[t, 1:2, :], (16, cap))
        col = jnp.broadcast_to(meta_ref[t, 2:3, :], (16, cap))
        tail = jnp.where(which == 0, row, jnp.where(which == 1, col, 0))
        out_ref[t, chan : chan + 16, :] = tail.astype(jnp.float32).astype(jnp.bfloat16)


def encode_all(points, meta, embed, mix, b_embed, b_mix):
    feat, point_num, slots = points.shape
    tiles, _, cap = meta.shape
    chan = mix.shape[0]
    mid = embed.shape[0]
    groups = HALF // PACK
    pick = (
        jnp.arange(HALF)[None, None, :]
        == PACK * jnp.arange(groups)[:, None, None] + jnp.arange(PACK)[None, :, None]
    )
    w1 = jnp.where(pick[:, :, None, None, :], embed[None, None, :, :, None], 0)
    w1 = w1.reshape(groups, PACK * mid, feat * HALF).astype(jnp.bfloat16)
    eye = jnp.eye(PACK, dtype=jnp.bool_)
    w2 = jnp.where(eye[:, None, :, None], mix[None, :, None, :], 0)
    w2 = w2.reshape(PACK * chan, PACK * mid).astype(jnp.bfloat16)
    b1 = jnp.tile(b_embed, PACK)[:, None]
    b2 = b_mix[:, None]
    step = 2
    return pl.pallas_call(
        functools.partial(encode_kernel, step),
        grid=(tiles // step,),
        in_specs=[
            pl.BlockSpec((feat, point_num, step * cap), lambda i: (0, 0, i)),
            pl.BlockSpec((step, 8, cap), lambda i: (i, 0, 0)),
            pl.BlockSpec(w1.shape, lambda i: (0, 0, 0)),
            pl.BlockSpec(w2.shape, lambda i: (0, 0)),
            pl.BlockSpec(b1.shape, lambda i: (0, 0)),
            pl.BlockSpec(b2.shape, lambda i: (0, 0)),
        ],
        out_specs=pl.BlockSpec((step, chan + 16, cap), lambda i: (i, 0, 0)),
        out_shape=jax.ShapeDtypeStruct((tiles, chan + 16, cap), jnp.bfloat16),
        name="encode",
    )(points, meta, w1, w2, b1, b2)


def scatter_kernel(cell_ref, vec_ref, out_ref, stage, *grids):
    tiles, _, cap = vec_ref.shape
    chan = out_ref.shape[1]
    for grid in grids:
        grid[...] = jnp.zeros_like(grid)

    def per_tile(t, carry):
        stage[...] = vec_ref[t, 0:chan, :].astype(jnp.float32).T
        unroll = 8

        def per_slot(s, inner):
            for k in range(unroll):
                cells = [cell_ref[t * cap + (s * unroll + k) * LANES + a] for a in range(LANES)]
                base = (s * unroll + k) * LANES
                olds = [grids[a][pl.ds(cells[a], 1), :] for a in range(LANES)]
                for a in range(LANES):
                    grids[a][pl.ds(cells[a], 1), :] = jnp.maximum(
                        olds[a], stage[pl.ds(base + a, 1), :]
                    )
            return inner

        return lax.fori_loop(0, cap // (LANES * unroll), per_slot, carry)

    lax.fori_loop(0, tiles, per_tile, 0)
    total = grids[0][...]
    for grid in grids[1:]:
        total = jnp.maximum(total, grid[...])
    out_ref[...] = total.astype(jnp.bfloat16)


def scatter_max(cells, vectors, chan):
    tiles, _, cap = vectors.shape
    area = ROWS_DEV * COLS_DEV
    return pl.pallas_call(
        scatter_kernel,
        in_specs=[
            pl.BlockSpec(memory_space=pltpu.SMEM),
            pl.BlockSpec(memory_space=pltpu.VMEM),
        ],
        out_specs=pl.BlockSpec(memory_space=pltpu.VMEM),
        out_shape=jax.ShapeDtypeStruct((area, chan), jnp.bfloat16),
        scratch_shapes=[pltpu.VMEM((cap, chan), jnp.float32)]
        + [pltpu.VMEM((area, chan), jnp.float32)] * LANES,
        name="scatter_max",
    )(cells, vectors)


def conv_valid(padded, kernel, bias_vec, stride):
    summed = lax.conv_general_dilated(
        padded[None],
        jnp.swapaxes(kernel, 2, 3),
        (stride, stride),
        "VALID",
        dimension_numbers=("NHWC", "HWIO", "NHWC"),
        preferred_element_type=jnp.float32,
    )[0]
    return jax.nn.relu(summed + bias_vec).astype(jnp.bfloat16)


def inside(block, edge):
    rows, cols, _ = block.shape
    own = (rows - 2 * edge, cols - 2 * edge)
    keep = None
    for dim, axis in enumerate(("row", "col")):
        place = lax.broadcasted_iota(jnp.int32, (rows, cols, 1), dim) - edge
        place = place + lax.axis_index(axis) * own[dim]
        good = (place >= 0) & (place < own[dim] * lax.axis_size(axis))
        keep = good if keep is None else keep & good
    return jnp.where(keep, block, jnp.zeros((), block.dtype))


def lift_layer(inputs, kernel, bias_vec):
    factor = kernel.shape[0]
    rows, cols, chan = inputs.shape
    if factor > 1:
        eye = jnp.eye(factor, dtype=jnp.bool_)
        wide = jnp.where(
            eye[None, None, :, :, None], inputs[:, :, None, None, :], jnp.zeros((), inputs.dtype)
        )
        wide = wide.reshape(rows, cols * factor, factor * chan)
    else:
        wide = inputs
    weight = jnp.transpose(kernel, (2, 0, 1, 3)).reshape(kernel.shape[2], factor, factor * chan)
    product = jnp.einsum("oak,ijk->oiaj", weight, wide, preferred_element_type=jnp.float32)
    product = product.reshape(kernel.shape[2], rows * factor, cols * factor)
    return jax.nn.relu(product + bias_vec[:, None, None]).astype(jnp.bfloat16)


def on_device(
    points,
    pillar_cell,
    point_count,
    tile_count,
    point_embed,
    point_mix,
    first_conv,
    second_conv,
    third_conv,
    fourth_conv,
    fifth_conv,
    sixth_conv,
    near_lift,
    mid_lift,
    far_lift,
    biases,
):
    extents = [
        point_embed.shape[0],
        point_mix.shape[0],
        first_conv.shape[2],
        second_conv.shape[2],
        third_conv.shape[2],
        fourth_conv.shape[2],
        fifth_conv.shape[2],
        sixth_conv.shape[2],
        near_lift.shape[2],
        mid_lift.shape[2],
        far_lift.shape[2],
    ]
    pieces = []
    offset = 0
    for extent in extents:
        pieces.append(biases[offset : offset + extent])
        offset += extent
    tile_num = tile_count.shape[0]
    capacity = points.shape[2] // tile_num
    ncols_all = COLS_DEV * lax.axis_size("col")
    live_slot = lax.broadcasted_iota(jnp.int32, (tile_num, capacity), 1) < tile_count[:, None]
    live_points = jnp.where(live_slot, point_count.reshape(tile_num, capacity), 0)
    row_local = (pillar_cell // ncols_all % ROWS_DEV).reshape(tile_num, capacity)
    col_local = (pillar_cell % COLS_DEV).reshape(tile_num, capacity)
    which = lax.broadcasted_iota(jnp.int32, (1, 8, 1), 1)
    meta = jnp.where(
        which == 0,
        live_points[:, None, :],
        jnp.where(which == 1, row_local[:, None, :], col_local[:, None, :]),
    )
    encoded = encode_all(points, meta, point_embed, point_mix, pieces[0], pieces[1])
    vectors = lax.all_to_all(encoded, ("row", "col"), split_axis=0, concat_axis=0, tiled=True)
    chan = point_mix.shape[0]
    place = vectors[:, chan : chan + 2, :].astype(jnp.int32)
    cells = (place[:, 0] * COLS_DEV + place[:, 1]).reshape(-1)
    bev = scatter_max(cells, vectors, chan).reshape(ROWS_DEV, COLS_DEV, chan)
    sides = (("row", 0), ("col", 1))
    level_one_a = inside(conv_valid(with_halo(bev, sides, 2, 2), first_conv, pieces[2], 1), 1)
    level_one = conv_valid(level_one_a, second_conv, pieces[3], 1)
    level_two_a = inside(conv_valid(with_halo(level_one, sides, 3, 2), third_conv, pieces[4], 2), 1)
    level_two = conv_valid(level_two_a, fourth_conv, pieces[5], 1)
    level_three_a = inside(
        conv_valid(with_halo(level_two, sides, 3, 2), fifth_conv, pieces[6], 2), 1
    )
    level_three = conv_valid(level_three_a, sixth_conv, pieces[7], 1)
    near = lift_layer(level_one, near_lift, pieces[8])
    middle = lift_layer(level_two, mid_lift, pieces[9])
    distant = lift_layer(level_three, far_lift, pieces[10])
    return jnp.concatenate([near, middle, distant], axis=0)


def solution(mesh):
    return jax.shard_map(
        on_device,
        mesh=mesh,
        in_specs=(
            P(None, None, ("slab", "row", "col")),
            P(("slab", "row", "col")),
            P(("slab", "row", "col")),
            P(("slab", "row", "col")),
            P(),
            P(),
            P(),
            P(),
            P(),
            P(),
            P(),
            P(),
            P(),
            P(),
            P(),
            P(),
        ),
        out_specs=P(None, ("slab", "row"), "col"),
        check_vma=False,
    )
```

```python
import functools

import jax
import jax.numpy as jnp
from jax import lax
from jax.experimental import pallas as pl
from jax.experimental.pallas import tpu as pltpu
from jax.sharding import PartitionSpec as P

ROWS_DEV = 16
COLS_DEV = 256
PACK = 4
HALF = 16
LANES = 4
SIDE = 16


def encode_kernel(tiles, x_ref, meta_ref, w1_ref, w2_ref, b1_ref, b2_ref, out_ref):
    chan = b2_ref.shape[0]
    cap = meta_ref.shape[2]
    points = x_ref.shape[1]
    feat = x_ref.shape[0]
    for t in range(tiles):
        count = meta_ref[t, 0:1, :]
        best = jnp.full((chan, cap), -jnp.inf, jnp.float32)
        for h in range(points // HALF):
            block = x_ref[:, h * HALF : (h + 1) * HALF, t * cap : (t + 1) * cap]
            block = block.reshape(feat * HALF, cap)
            for q in range(HALF // PACK):
                hidden = jnp.dot(w1_ref[q], block, preferred_element_type=jnp.float32)
                hidden = jnp.maximum(hidden + b1_ref[...], 0.0).astype(jnp.bfloat16)
                second = jnp.dot(w2_ref[...], hidden, preferred_element_type=jnp.float32)
                for p in range(PACK):
                    j = h * HALF + q * PACK + p
                    part = second[p * chan : (p + 1) * chan]
                    best = jnp.maximum(best, jnp.where(count > j, part, -jnp.inf))
        vec = jnp.maximum(best + b2_ref[...], 0.0)
        out_ref[t, 0:chan, :] = vec.astype(jnp.bfloat16)
        which = lax.broadcasted_iota(jnp.int32, (16, cap), 0)
        row = jnp.broadcast_to(meta_ref[t, 1:2, :], (16, cap))
        col = jnp.broadcast_to(meta_ref[t, 2:3, :], (16, cap))
        tail = jnp.where(which == 0, row, jnp.where(which == 1, col, 0))
        out_ref[t, chan : chan + 16, :] = tail.astype(jnp.float32).astype(jnp.bfloat16)


def encode_all(points, meta, embed, mix, b_embed, b_mix):
    feat, point_num, slots = points.shape
    tiles, _, cap = meta.shape
    chan = mix.shape[0]
    mid = embed.shape[0]
    groups = HALF // PACK
    pick = (
        jnp.arange(HALF)[None, None, :]
        == PACK * jnp.arange(groups)[:, None, None] + jnp.arange(PACK)[None, :, None]
    )
    w1 = jnp.where(pick[:, :, None, None, :], embed[None, None, :, :, None], 0)
    w1 = w1.reshape(groups, PACK * mid, feat * HALF).astype(jnp.bfloat16)
    eye = jnp.eye(PACK, dtype=jnp.bool_)
    w2 = jnp.where(eye[:, None, :, None], mix[None, :, None, :], 0)
    w2 = w2.reshape(PACK * chan, PACK * mid).astype(jnp.bfloat16)
    b1 = jnp.tile(b_embed, PACK)[:, None]
    b2 = b_mix[:, None]
    step = 2
    return pl.pallas_call(
        functools.partial(encode_kernel, step),
        grid=(tiles // step,),
        in_specs=[
            pl.BlockSpec((feat, point_num, step * cap), lambda i: (0, 0, i)),
            pl.BlockSpec((step, 8, cap), lambda i: (i, 0, 0)),
            pl.BlockSpec(w1.shape, lambda i: (0, 0, 0)),
            pl.BlockSpec(w2.shape, lambda i: (0, 0)),
            pl.BlockSpec(b1.shape, lambda i: (0, 0)),
            pl.BlockSpec(b2.shape, lambda i: (0, 0)),
        ],
        out_specs=pl.BlockSpec((step, chan + 16, cap), lambda i: (i, 0, 0)),
        out_shape=jax.ShapeDtypeStruct((tiles, chan + 16, cap), jnp.bfloat16),
        name="encode",
    )(points, meta, w1, w2, b1, b2)


def scatter_kernel(cell_ref, vec_ref, out_ref, stage, *grids):
    tiles, _, cap = vec_ref.shape
    chan = out_ref.shape[1]
    for grid in grids:
        grid[...] = jnp.zeros_like(grid)

    def per_tile(t, carry):
        stage[...] = vec_ref[t, 0:chan, :].astype(jnp.float32).T
        unroll = 8

        def per_slot(s, inner):
            for k in range(unroll):
                cells = [cell_ref[t * cap + (s * unroll + k) * LANES + a] for a in range(LANES)]
                base = (s * unroll + k) * LANES
                olds = [grids[a][pl.ds(cells[a], 1), :] for a in range(LANES)]
                for a in range(LANES):
                    grids[a][pl.ds(cells[a], 1), :] = jnp.maximum(
                        olds[a], stage[pl.ds(base + a, 1), :]
                    )
            return inner

        return lax.fori_loop(0, cap // (LANES * unroll), per_slot, carry)

    lax.fori_loop(0, tiles, per_tile, 0)
    total = grids[0][...]
    for grid in grids[1:]:
        total = jnp.maximum(total, grid[...])
    out_ref[...] = total.astype(jnp.bfloat16)


def scatter_max(cells, vectors, chan):
    tiles, _, cap = vectors.shape
    area = ROWS_DEV * COLS_DEV
    return pl.pallas_call(
        scatter_kernel,
        in_specs=[
            pl.BlockSpec(memory_space=pltpu.SMEM),
            pl.BlockSpec(memory_space=pltpu.VMEM),
        ],
        out_specs=pl.BlockSpec(memory_space=pltpu.VMEM),
        out_shape=jax.ShapeDtypeStruct((area, chan), jnp.bfloat16),
        scratch_shapes=[pltpu.VMEM((cap, chan), jnp.float32)]
        + [pltpu.VMEM((area, chan), jnp.float32)] * LANES,
        name="scatter_max",
    )(cells, vectors)


def around(count_rows, count_cols):
    return [
        (dr, dc)
        for dr in (-1, 0, 1)
        for dc in (-1, 0, 1)
        if (dr, dc) != (0, 0) and (dr == 0 or count_rows > 1) and (dc == 0 or count_cols > 1)
    ]


def span_of(step, before, size, after):
    if step > 0:
        return slice(size - before, size), slice(0, before)
    if step < 0:
        return slice(0, after), slice(before + size, before + size + after)
    return slice(0, size), slice(before, before + size)


def halo_kernel(before, after, x_ref, ext_ref, send_sem, recv_sem):
    rows, cols, chan = x_ref.shape
    count_rows, count_cols = lax.axis_size("row"), lax.axis_size("col")
    my_row, my_col = lax.axis_index("row"), lax.axis_index("col")
    steps = around(count_rows, count_cols)

    def exists(dr, dc):
        row, col = my_row + dr, my_col + dc
        return (row >= 0) & (row < count_rows) & (col >= 0) & (col < count_cols)

    barrier = pltpu.get_barrier_semaphore()
    for dr, dc in steps:

        @pl.when(exists(dr, dc))
        def _():
            pl.semaphore_signal(
                barrier,
                inc=1,
                device_id={"row": my_row + dr, "col": my_col + dc},
                device_id_type=pl.DeviceIdType.MESH,
            )

    peers = sum(jnp.where(exists(dr, dc), 1, 0) for dr, dc in steps)
    pl.semaphore_wait(barrier, peers)

    def copy_of(place):
        dr, dc = steps[place]
        row_from, row_to = span_of(dr, before, rows, after)
        col_from, col_to = span_of(dc, SIDE, cols, SIDE)
        return pltpu.make_async_remote_copy(
            src_ref=x_ref.at[row_from, col_from, :],
            dst_ref=ext_ref.at[row_to, col_to, :],
            send_sem=send_sem.at[place],
            recv_sem=recv_sem.at[place],
            device_id={"row": my_row + dr, "col": my_col + dc},
            device_id_type=pl.DeviceIdType.MESH,
        )

    for place, (dr, dc) in enumerate(steps):

        @pl.when(exists(dr, dc))
        def _():
            copy_of(place).start()

    ext_ref[before : before + rows, SIDE : SIDE + cols, :] = x_ref[...]
    for dr in (-1, 0, 1):
        for dc in (-1, 0, 1):
            if (dr, dc) == (0, 0):
                continue
            row_to = span_of(dr, before, rows, after)[1]
            col_to = span_of(dc, SIDE, cols, SIDE)[1]
            shape = (row_to.stop - row_to.start, col_to.stop - col_to.start, chan)

            @pl.when(jnp.logical_not(exists(-dr, -dc)))
            def _():
                ext_ref[row_to, col_to, :] = jnp.zeros(shape, ext_ref.dtype)

    for place, (dr, dc) in enumerate(steps):

        @pl.when(exists(dr, dc))
        def _():
            copy_of(place).wait_send()

        @pl.when(exists(-dr, -dc))
        def _():
            copy_of(place).wait_recv()


def with_halo(block, before, after, call_id):
    rows, cols, chan = block.shape
    count = len(around(lax.axis_size("row"), lax.axis_size("col")))
    return pl.pallas_call(
        functools.partial(halo_kernel, before, after),
        in_specs=[pl.BlockSpec(memory_space=pltpu.VMEM)],
        out_specs=pl.BlockSpec(memory_space=pltpu.VMEM),
        out_shape=jax.ShapeDtypeStruct(
            (rows + before + after, cols + 2 * SIDE, chan), block.dtype
        ),
        scratch_shapes=[
            pltpu.SemaphoreType.DMA((count,)),
            pltpu.SemaphoreType.DMA((count,)),
        ],
        compiler_params=pltpu.CompilerParams(collective_id=call_id, has_side_effects=True),
        name=f"halo_{call_id}",
    )(block)


def level_kernel(
    stride, ext_ref, wa_ref, wb_ref, ba_ref, bb_ref, out_ref, ta, tb, stage_a, cat_a, stage_b, cat_b
):
    ext_rows, ext_cols, chan_in = ext_ref.shape
    rows, cols, chan = out_ref.shape
    mid_rows, mid_cols, _ = cat_b.shape
    edge = SIDE // stride
    for w_ref, t_ref in ((wa_ref, ta), (wb_ref, tb)):
        deep = w_ref.shape[3]
        for u in range(3):
            for v in range(3):
                flip = w_ref[u, v].astype(jnp.float32).T
                t_ref[u, v * deep : (v + 1) * deep, :] = flip.astype(jnp.bfloat16)
    for stage in (stage_a, stage_b):
        stage[0:8, :] = jnp.zeros((8, stage.shape[1]), jnp.float32)
        stage[stage.shape[0] - 8 :, :] = jnp.zeros((8, stage.shape[1]), jnp.float32)

    def gather(stage, values, count, step):
        stage[8 : 8 + values.shape[0], :] = values
        if step == 1:
            parts = [stage[7 + v : 7 + v + count, :] for v in range(3)]
        else:
            parts = [stage[pl.ds(7 + v, count, stride=step), :] for v in range(3)]
        return jnp.concatenate(parts, axis=1).astype(jnp.bfloat16)

    def first(r, carry):
        cat_a[r] = gather(stage_a, ext_ref[r].astype(jnp.float32), mid_cols, stride)
        return carry

    lax.fori_loop(0, ext_rows, first, 0)

    col = lax.broadcasted_iota(jnp.int32, (mid_cols, chan), 0) - edge
    col = col + lax.axis_index("col") * cols
    col_good = (col >= 0) & (col < cols * lax.axis_size("col"))
    row_base = lax.axis_index("row") * rows
    row_limit = rows * lax.axis_size("row")

    def second(i, carry):
        total = jnp.broadcast_to(ba_ref[...], (mid_cols, chan))
        for u in range(3):
            total = total + jnp.dot(
                cat_a[stride * i + u], ta[u], preferred_element_type=jnp.float32
            )
        total = jnp.maximum(total, 0.0).astype(jnp.bfloat16).astype(jnp.float32)
        row = row_base + i - 1
        total = jnp.where(col_good & (row >= 0) & (row < row_limit), total, 0.0)
        cat_b[i] = gather(stage_b, total, mid_cols, 1)
        return carry

    lax.fori_loop(0, mid_rows, second, 0)

    def third(i, carry):
        total = jnp.broadcast_to(bb_ref[...], (mid_cols, chan))
        for u in range(3):
            total = total + jnp.dot(cat_b[i + u], tb[u], preferred_element_type=jnp.float32)
        total = jnp.maximum(total, 0.0)
        out_ref[i] = total[edge : edge + cols].astype(jnp.bfloat16)
        return carry

    lax.fori_loop(0, rows, third, 0)


def level(block, kernel_a, kernel_b, bias_a, bias_b, stride, call_id):
    rows, cols, chan_in = block.shape
    before, after = (2, 2) if stride == 1 else (3, 2)
    ext = with_halo(block, before, after, call_id)
    chan = kernel_a.shape[2]
    rows_out, cols_out = rows // stride, cols // stride
    mid_rows, mid_cols = rows_out + 2, ext.shape[1] // stride
    vmem = pl.BlockSpec(memory_space=pltpu.VMEM)
    return pl.pallas_call(
        functools.partial(level_kernel, stride),
        in_specs=[vmem] * 5,
        out_specs=vmem,
        out_shape=jax.ShapeDtypeStruct((rows_out, cols_out, chan), jnp.bfloat16),
        scratch_shapes=[
            pltpu.VMEM((3, 3 * chan_in, chan), jnp.bfloat16),
            pltpu.VMEM((3, 3 * chan, chan), jnp.bfloat16),
            pltpu.VMEM((ext.shape[1] + 16, chan_in), jnp.float32),
            pltpu.VMEM((ext.shape[0], mid_cols, 3 * chan_in), jnp.bfloat16),
            pltpu.VMEM((mid_cols + 16, chan), jnp.float32),
            pltpu.VMEM((mid_rows, mid_cols, 3 * chan), jnp.bfloat16),
        ],
        name=f"level_{call_id}",
    )(ext, kernel_a, kernel_b, bias_a[None], bias_b[None])


def lift_layer(inputs, kernel, bias_vec):
    factor = kernel.shape[0]
    rows, cols, chan = inputs.shape
    if factor > 1:
        eye = jnp.eye(factor, dtype=jnp.bool_)
        wide = jnp.where(
            eye[None, None, :, :, None], inputs[:, :, None, None, :], jnp.zeros((), inputs.dtype)
        )
        wide = wide.reshape(rows, cols * factor, factor * chan)
    else:
        wide = inputs
    weight = jnp.transpose(kernel, (2, 0, 1, 3)).reshape(kernel.shape[2], factor, factor * chan)
    product = jnp.einsum("oak,ijk->oiaj", weight, wide, preferred_element_type=jnp.float32)
    product = product.reshape(kernel.shape[2], rows * factor, cols * factor)
    return jax.nn.relu(product + bias_vec[:, None, None]).astype(jnp.bfloat16)


def on_device(
    points,
    pillar_cell,
    point_count,
    tile_count,
    point_embed,
    point_mix,
    first_conv,
    second_conv,
    third_conv,
    fourth_conv,
    fifth_conv,
    sixth_conv,
    near_lift,
    mid_lift,
    far_lift,
    biases,
):
    extents = [
        point_embed.shape[0],
        point_mix.shape[0],
        first_conv.shape[2],
        second_conv.shape[2],
        third_conv.shape[2],
        fourth_conv.shape[2],
        fifth_conv.shape[2],
        sixth_conv.shape[2],
        near_lift.shape[2],
        mid_lift.shape[2],
        far_lift.shape[2],
    ]
    pieces = []
    offset = 0
    for extent in extents:
        pieces.append(biases[offset : offset + extent])
        offset += extent
    tile_num = tile_count.shape[0]
    capacity = points.shape[2] // tile_num
    ncols_all = COLS_DEV * lax.axis_size("col")
    live_slot = lax.broadcasted_iota(jnp.int32, (tile_num, capacity), 1) < tile_count[:, None]
    live_points = jnp.where(live_slot, point_count.reshape(tile_num, capacity), 0)
    row_local = (pillar_cell // ncols_all % ROWS_DEV).reshape(tile_num, capacity)
    col_local = (pillar_cell % COLS_DEV).reshape(tile_num, capacity)
    which = lax.broadcasted_iota(jnp.int32, (1, 8, 1), 1)
    meta = jnp.where(
        which == 0,
        live_points[:, None, :],
        jnp.where(which == 1, row_local[:, None, :], col_local[:, None, :]),
    )
    encoded = encode_all(points, meta, point_embed, point_mix, pieces[0], pieces[1])
    vectors = lax.all_to_all(encoded, ("row", "col"), split_axis=0, concat_axis=0, tiled=True)
    chan = point_mix.shape[0]
    place = vectors[:, chan : chan + 2, :].astype(jnp.int32)
    cells = (place[:, 0] * COLS_DEV + place[:, 1]).reshape(-1)
    bev = scatter_max(cells, vectors, chan).reshape(ROWS_DEV, COLS_DEV, chan)
    level_one = level(bev, first_conv, second_conv, pieces[2], pieces[3], 1, 0)
    level_two = level(level_one, third_conv, fourth_conv, pieces[4], pieces[5], 2, 1)
    level_three = level(level_two, fifth_conv, sixth_conv, pieces[6], pieces[7], 2, 2)
    near = lift_layer(level_one, near_lift, pieces[8])
    middle = lift_layer(level_two, mid_lift, pieces[9])
    distant = lift_layer(level_three, far_lift, pieces[10])
    return jnp.concatenate([near, middle, distant], axis=0)


def solution(mesh):
    return jax.shard_map(
        on_device,
        mesh=mesh,
        in_specs=(
            P(None, None, ("slab", "row", "col")),
            P(("slab", "row", "col")),
            P(("slab", "row", "col")),
            P(("slab", "row", "col")),
            P(),
            P(),
            P(),
            P(),
            P(),
            P(),
            P(),
            P(),
            P(),
            P(),
            P(),
            P(),
        ),
        out_specs=P(None, ("slab", "row"), "col"),
        check_vma=False,
    )
```

```python
import functools

import jax
import jax.numpy as jnp
from jax import lax
from jax.experimental import pallas as pl
from jax.experimental.pallas import tpu as pltpu
from jax.sharding import PartitionSpec as P

ROWS_DEV = 16
COLS_DEV = 256
PACK = 4
HALF = 16
LANES = 4
SIDE = 16
TILE = 128


def prepare_kernel(embed_ref, mix_ref, bias_ref, w1_ref, w2_ref, b1_ref, b2_ref):
    mid, feat = embed_ref.shape
    chan = mix_ref.shape[0]
    wide = w1_ref.shape[2]
    lane = lax.broadcasted_iota(jnp.int32, (feat, wide), 1)
    spread = lane // HALF == lax.broadcasted_iota(jnp.int32, (feat, wide), 0)
    spread = jnp.where(spread, 1.0, 0.0).astype(jnp.bfloat16)
    full = jnp.dot(embed_ref[...], spread, preferred_element_type=jnp.float32)
    point = lax.broadcasted_iota(jnp.int32, (mid, wide), 1) % HALF
    for q in range(HALF // PACK):
        for p in range(PACK):
            part = jnp.where(point == q * PACK + p, full, 0.0)
            w1_ref[q, p * mid : (p + 1) * mid, :] = part.astype(jnp.bfloat16)
    w2_ref[...] = jnp.zeros_like(w2_ref)
    for p in range(PACK):
        w2_ref[p * chan : (p + 1) * chan, p * mid : (p + 1) * mid] = mix_ref[...]
    both = mid + chan
    column = jnp.broadcast_to(bias_ref[...], (both, both)).T[:, 0:1]
    for p in range(PACK):
        b1_ref[p * mid : (p + 1) * mid, :] = column[0:mid]
    b2_ref[...] = column[mid:both]


def encode_kernel(x_ref, meta_ref, w1_ref, w2_ref, b1_ref, b2_ref, out_ref, send_ref, ssem, rsem):
    feat, points, _ = x_ref.shape
    tiles, _, cap = meta_ref.shape
    chan = b2_ref.shape[0]
    col_count = lax.axis_size("col")
    me = lax.axis_index("row") * col_count + lax.axis_index("col")

    def device_of(tile):
        return {"row": tile // col_count, "col": tile % col_count}

    def encode(tile, dest_ref):
        count = meta_ref[tile, 0:1, :]
        start = pl.multiple_of(tile * cap, cap)
        best = jnp.full((chan, cap), -jnp.inf, jnp.float32)
        for h in range(points // HALF):
            block = x_ref[:, h * HALF : (h + 1) * HALF, pl.ds(start, cap)]
            block = block.reshape(feat * HALF, cap)
            for q in range(HALF // PACK):
                hidden = jnp.dot(w1_ref[q], block, preferred_element_type=jnp.float32)
                hidden = jnp.maximum(hidden + b1_ref[...], 0.0).astype(jnp.bfloat16)
                second = jnp.dot(w2_ref[...], hidden, preferred_element_type=jnp.float32)
                for p in range(PACK):
                    j = h * HALF + q * PACK + p
                    part = second[p * chan : (p + 1) * chan]
                    best = jnp.maximum(best, jnp.where(count > j, part, -jnp.inf))
        vec = jnp.maximum(best + b2_ref[...], 0.0)
        dest_ref[tile, 0:chan, :] = vec.astype(jnp.bfloat16)
        which = lax.broadcasted_iota(jnp.int32, (16, cap), 0)
        row = jnp.broadcast_to(meta_ref[tile, 1:2, :], (16, cap))
        col = jnp.broadcast_to(meta_ref[tile, 2:3, :], (16, cap))
        tail = jnp.where(which == 0, row, jnp.where(which == 1, col, 0))
        dest_ref[tile, chan : chan + 16, :] = tail.astype(jnp.float32).astype(jnp.bfloat16)

    def copy_of(i, slot):
        tile = (me + i) % tiles
        return pltpu.make_async_remote_copy(
            src_ref=send_ref.at[tile],
            dst_ref=out_ref.at[slot],
            send_sem=ssem.at[i],
            recv_sem=rsem.at[i],
            device_id=device_of(tile),
            device_id_type=pl.DeviceIdType.MESH,
        )

    barrier = pltpu.get_barrier_semaphore()

    def greet(i, carry):
        pl.semaphore_signal(
            barrier,
            inc=1,
            device_id=device_of((me + i) % tiles),
            device_id_type=pl.DeviceIdType.MESH,
        )
        return carry

    lax.fori_loop(1, tiles, greet, 0)
    pl.semaphore_wait(barrier, tiles - 1)

    def step(i, carry):
        encode((me + i) % tiles, send_ref)
        copy_of(i, me).start()
        return carry

    lax.fori_loop(1, tiles, step, 0)
    encode(me, out_ref)

    def finish(i, carry):
        copy_of(i, me).wait_send()
        copy_of(i, (me - i + tiles) % tiles).wait_recv()
        return carry

    lax.fori_loop(1, tiles, finish, 0)


def encode_all(points, meta, embed, mix, bias):
    feat = points.shape[0]
    tiles, _, cap = meta.shape
    mid, chan = embed.shape[0], mix.shape[0]
    vmem = pl.BlockSpec(memory_space=pltpu.VMEM)
    weights = pl.pallas_call(
        prepare_kernel,
        in_specs=[vmem] * 3,
        out_specs=[vmem] * 4,
        out_shape=[
            jax.ShapeDtypeStruct((HALF // PACK, PACK * mid, feat * HALF), jnp.bfloat16),
            jax.ShapeDtypeStruct((PACK * chan, PACK * mid), jnp.bfloat16),
            jax.ShapeDtypeStruct((PACK * mid, 1), jnp.float32),
            jax.ShapeDtypeStruct((chan, 1), jnp.float32),
        ],
        name="prepare",
    )(embed, mix, bias)
    return pl.pallas_call(
        encode_kernel,
        in_specs=[vmem] * 6,
        out_specs=vmem,
        out_shape=jax.ShapeDtypeStruct((tiles, chan + 16, cap), jnp.bfloat16),
        scratch_shapes=[
            pltpu.VMEM((tiles, chan + 16, cap), jnp.bfloat16),
            pltpu.SemaphoreType.DMA((tiles,)),
            pltpu.SemaphoreType.DMA((tiles,)),
        ],
        compiler_params=pltpu.CompilerParams(collective_id=7, has_side_effects=True),
        name="encode_send",
    )(points, meta, *weights)


def scatter_kernel(cell_ref, vec_ref, out_ref, stage, *grids):
    tiles, _, cap = vec_ref.shape
    chan = out_ref.shape[1]
    for grid in grids:
        grid[...] = jnp.zeros_like(grid)

    def per_tile(t, carry):
        stage[...] = vec_ref[t, 0:chan, :].astype(jnp.float32).T
        unroll = 8

        def per_slot(s, inner):
            for k in range(unroll):
                cells = [cell_ref[t * cap + (s * unroll + k) * LANES + a] for a in range(LANES)]
                base = (s * unroll + k) * LANES
                olds = [grids[a][pl.ds(cells[a], 1), :] for a in range(LANES)]
                for a in range(LANES):
                    grids[a][pl.ds(cells[a], 1), :] = jnp.maximum(
                        olds[a], stage[pl.ds(base + a, 1), :]
                    )
            return inner

        return lax.fori_loop(0, cap // (LANES * unroll), per_slot, carry)

    lax.fori_loop(0, tiles, per_tile, 0)
    total = grids[0][...]
    for grid in grids[1:]:
        total = jnp.maximum(total, grid[...])
    out_ref[...] = total.astype(jnp.bfloat16)


def scatter_max(cells, vectors, chan):
    tiles, _, cap = vectors.shape
    area = ROWS_DEV * COLS_DEV
    return pl.pallas_call(
        scatter_kernel,
        in_specs=[
            pl.BlockSpec(memory_space=pltpu.SMEM),
            pl.BlockSpec(memory_space=pltpu.VMEM),
        ],
        out_specs=pl.BlockSpec(memory_space=pltpu.VMEM),
        out_shape=jax.ShapeDtypeStruct((area, chan), jnp.bfloat16),
        scratch_shapes=[pltpu.VMEM((cap, chan), jnp.float32)]
        + [pltpu.VMEM((area, chan), jnp.float32)] * LANES,
        name="scatter_max",
    )(cells, vectors)


def around(count_rows, count_cols):
    return [
        (dr, dc)
        for dr in (-1, 0, 1)
        for dc in (-1, 0, 1)
        if (dr, dc) != (0, 0) and (dr == 0 or count_rows > 1) and (dc == 0 or count_cols > 1)
    ]


def span_of(step, before, size, after):
    if step > 0:
        return slice(size - before, size), slice(0, before)
    if step < 0:
        return slice(0, after), slice(before + size, before + size + after)
    return slice(0, size), slice(before, before + size)


def halo_kernel(before, after, x_ref, ext_ref, send_sem, recv_sem):
    rows, cols, chan = x_ref.shape
    count_rows, count_cols = lax.axis_size("row"), lax.axis_size("col")
    my_row, my_col = lax.axis_index("row"), lax.axis_index("col")
    steps = around(count_rows, count_cols)

    def exists(dr, dc):
        row, col = my_row + dr, my_col + dc
        return (row >= 0) & (row < count_rows) & (col >= 0) & (col < count_cols)

    barrier = pltpu.get_barrier_semaphore()
    for dr, dc in steps:

        @pl.when(exists(dr, dc))
        def _():
            pl.semaphore_signal(
                barrier,
                inc=1,
                device_id={"row": my_row + dr, "col": my_col + dc},
                device_id_type=pl.DeviceIdType.MESH,
            )

    peers = sum(jnp.where(exists(dr, dc), 1, 0) for dr, dc in steps)
    pl.semaphore_wait(barrier, peers)

    def copy_of(place):
        dr, dc = steps[place]
        row_from, row_to = span_of(dr, before, rows, after)
        col_from, col_to = span_of(dc, SIDE, cols, SIDE)
        return pltpu.make_async_remote_copy(
            src_ref=x_ref.at[row_from, col_from, :],
            dst_ref=ext_ref.at[row_to, col_to, :],
            send_sem=send_sem.at[place],
            recv_sem=recv_sem.at[place],
            device_id={"row": my_row + dr, "col": my_col + dc},
            device_id_type=pl.DeviceIdType.MESH,
        )

    for place, (dr, dc) in enumerate(steps):

        @pl.when(exists(dr, dc))
        def _():
            copy_of(place).start()

    ext_ref[before : before + rows, SIDE : SIDE + cols, :] = x_ref[...]
    for dr in (-1, 0, 1):
        for dc in (-1, 0, 1):
            if (dr, dc) == (0, 0):
                continue
            row_to = span_of(dr, before, rows, after)[1]
            col_to = span_of(dc, SIDE, cols, SIDE)[1]
            shape = (row_to.stop - row_to.start, col_to.stop - col_to.start, chan)

            @pl.when(jnp.logical_not(exists(-dr, -dc)))
            def _():
                ext_ref[row_to, col_to, :] = jnp.zeros(shape, ext_ref.dtype)

    for place, (dr, dc) in enumerate(steps):

        @pl.when(exists(dr, dc))
        def _():
            copy_of(place).wait_send()

        @pl.when(exists(-dr, -dc))
        def _():
            copy_of(place).wait_recv()


def with_halo(block, before, after, call_id):
    rows, cols, chan = block.shape
    count = len(around(lax.axis_size("row"), lax.axis_size("col")))
    return pl.pallas_call(
        functools.partial(halo_kernel, before, after),
        in_specs=[pl.BlockSpec(memory_space=pltpu.VMEM)],
        out_specs=pl.BlockSpec(memory_space=pltpu.VMEM),
        out_shape=jax.ShapeDtypeStruct(
            (rows + before + after, cols + 2 * SIDE, chan), block.dtype
        ),
        scratch_shapes=[
            pltpu.SemaphoreType.DMA((count,)),
            pltpu.SemaphoreType.DMA((count,)),
        ],
        compiler_params=pltpu.CompilerParams(collective_id=call_id, has_side_effects=True),
        name=f"halo_{call_id}",
    )(block)


def level_kernel(
    stride, factor, ext_ref, wa_ref, wb_ref, ba_ref, bb_ref, out_ref, wide_ref,
    ta, tb, stage_a, cat_a, stage_b, cat_b, wide
):
    ext_rows, ext_cols, chan_in = ext_ref.shape
    rows, cols, chan = out_ref.shape
    mid_rows, mid_cols, _ = cat_b.shape
    edge = SIDE // stride
    for w_ref, t_ref in ((wa_ref, ta), (wb_ref, tb)):
        deep = w_ref.shape[3]
        for u in range(3):
            for v in range(3):
                flip = w_ref[u, v].astype(jnp.float32).T
                t_ref[u, v * deep : (v + 1) * deep, :] = flip.astype(jnp.bfloat16)
    for stage in (stage_a, stage_b):
        stage[0:8, :] = jnp.zeros((8, stage.shape[1]), jnp.float32)
        stage[stage.shape[0] - 8 :, :] = jnp.zeros((8, stage.shape[1]), jnp.float32)

    wide[...] = jnp.zeros_like(wide)

    def gather(stage, values, count, step):
        stage[8 : 8 + values.shape[0], :] = values
        if step == 1:
            parts = [stage[7 + v : 7 + v + count, :] for v in range(3)]
        else:
            parts = [stage[pl.ds(7 + v, count, stride=step), :] for v in range(3)]
        return jnp.concatenate(parts, axis=1).astype(jnp.bfloat16)

    def first(r, carry):
        cat_a[r] = gather(stage_a, ext_ref[r].astype(jnp.float32), mid_cols, stride)
        return carry

    lax.fori_loop(0, ext_rows, first, 0, unroll=2)

    col = lax.broadcasted_iota(jnp.int32, (mid_cols, chan), 0) - edge
    col = col + lax.axis_index("col") * cols
    col_good = (col >= 0) & (col < cols * lax.axis_size("col"))
    row_base = lax.axis_index("row") * rows
    row_limit = rows * lax.axis_size("row")

    def second(i, carry):
        total = jnp.broadcast_to(ba_ref[...], (mid_cols, chan))
        for u in range(3):
            total = total + jnp.dot(
                cat_a[stride * i + u], ta[u], preferred_element_type=jnp.float32
            )
        total = jnp.maximum(total, 0.0).astype(jnp.bfloat16).astype(jnp.float32)
        row = row_base + i - 1
        total = jnp.where(col_good & (row >= 0) & (row < row_limit), total, 0.0)
        cat_b[i] = gather(stage_b, total, mid_cols, 1)
        return carry

    lax.fori_loop(0, mid_rows, second, 0, unroll=2)

    def third(i, carry):
        total = jnp.broadcast_to(bb_ref[...], (mid_cols, chan))
        for u in range(3):
            total = total + jnp.dot(cat_b[i + u], tb[u], preferred_element_type=jnp.float32)
        total = jnp.maximum(total, 0.0)
        total = total[edge : edge + cols]
        out_ref[i] = total.astype(jnp.bfloat16)
        if factor > 1:
            parts = chan // TILE
            for b in range(factor):
                for k in range(parts):
                    piece = total[:, k * TILE : (k + 1) * TILE]
                    wide[b * parts + k, pl.ds(b, cols, stride=factor), :] = piece
            for k in range(factor * parts):
                wide_ref[i, :, k * TILE : (k + 1) * TILE] = wide[k].astype(jnp.bfloat16)
        return carry

    lax.fori_loop(0, rows, third, 0, unroll=2)


def level(block, kernel_a, kernel_b, bias_a, bias_b, stride, factor, call_id):
    rows, cols, chan_in = block.shape
    before, after = (2, 2) if stride == 1 else (3, 2)
    ext = with_halo(block, before, after, call_id)
    chan = kernel_a.shape[2]
    rows_out, cols_out = rows // stride, cols // stride
    mid_rows, mid_cols = rows_out + 2, ext.shape[1] // stride
    vmem = pl.BlockSpec(memory_space=pltpu.VMEM)
    wide_shape = (rows_out, cols_out * factor, chan * factor) if factor > 1 else (1, 16, 128)
    return pl.pallas_call(
        functools.partial(level_kernel, stride, factor),
        in_specs=[vmem] * 5,
        out_specs=[vmem, vmem],
        out_shape=[
            jax.ShapeDtypeStruct((rows_out, cols_out, chan), jnp.bfloat16),
            jax.ShapeDtypeStruct(wide_shape, jnp.bfloat16),
        ],
        scratch_shapes=[
            pltpu.VMEM((3, 3 * chan_in, chan), jnp.bfloat16),
            pltpu.VMEM((3, 3 * chan, chan), jnp.bfloat16),
            pltpu.VMEM((ext.shape[1] + 16, chan_in), jnp.float32),
            pltpu.VMEM((ext.shape[0], mid_cols, 3 * chan_in), jnp.bfloat16),
            pltpu.VMEM((mid_cols + 16, chan), jnp.float32),
            pltpu.VMEM((mid_rows, mid_cols, 3 * chan), jnp.bfloat16),
            pltpu.VMEM((factor * chan // TILE, cols_out * factor, TILE) if factor > 1 else (1, 8, TILE), jnp.float32),
        ],
        name=f"level_{call_id}",
    )(ext, kernel_a, kernel_b, bias_a[None], bias_b[None])


def lift_layer(wide, kernel, bias_vec):
    factor = kernel.shape[0]
    rows, cols, depth = wide.shape
    weight = jnp.transpose(kernel, (2, 0, 1, 3)).reshape(kernel.shape[2], factor, depth)
    product = jnp.einsum("oak,ijk->oiaj", weight, wide, preferred_element_type=jnp.float32)
    product = product.reshape(kernel.shape[2], rows * factor, cols)
    return jax.nn.relu(product + bias_vec[:, None, None]).astype(jnp.bfloat16)


def on_device(
    points,
    pillar_cell,
    point_count,
    tile_count,
    point_embed,
    point_mix,
    first_conv,
    second_conv,
    third_conv,
    fourth_conv,
    fifth_conv,
    sixth_conv,
    near_lift,
    mid_lift,
    far_lift,
    biases,
):
    extents = [
        point_embed.shape[0],
        point_mix.shape[0],
        first_conv.shape[2],
        second_conv.shape[2],
        third_conv.shape[2],
        fourth_conv.shape[2],
        fifth_conv.shape[2],
        sixth_conv.shape[2],
        near_lift.shape[2],
        mid_lift.shape[2],
        far_lift.shape[2],
    ]
    pieces = []
    offset = 0
    for extent in extents:
        pieces.append(biases[offset : offset + extent])
        offset += extent
    tile_num = tile_count.shape[0]
    capacity = points.shape[2] // tile_num
    ncols_all = COLS_DEV * lax.axis_size("col")
    live_slot = lax.broadcasted_iota(jnp.int32, (tile_num, capacity), 1) < tile_count[:, None]
    live_points = jnp.where(live_slot, point_count.reshape(tile_num, capacity), 0)
    row_local = (pillar_cell // ncols_all % ROWS_DEV).reshape(tile_num, capacity)
    col_local = (pillar_cell % COLS_DEV).reshape(tile_num, capacity)
    which = lax.broadcasted_iota(jnp.int32, (1, 8, 1), 1)
    meta = jnp.where(
        which == 0,
        live_points[:, None, :],
        jnp.where(which == 1, row_local[:, None, :], col_local[:, None, :]),
    )
    lead = biases[: extents[0] + extents[1]].reshape(1, -1)
    vectors = encode_all(points, meta, point_embed, point_mix, lead)
    chan = point_mix.shape[0]
    place = vectors[:, chan : chan + 2, :].astype(jnp.int32)
    cells = (place[:, 0] * COLS_DEV + place[:, 1]).reshape(-1)
    bev = scatter_max(cells, vectors, chan).reshape(ROWS_DEV, COLS_DEV, chan)
    level_one, _ = level(bev, first_conv, second_conv, pieces[2], pieces[3], 1, 1, 0)
    level_two, wide_two = level(
        level_one, third_conv, fourth_conv, pieces[4], pieces[5], 2, mid_lift.shape[0], 1
    )
    _, wide_three = level(
        level_two, fifth_conv, sixth_conv, pieces[6], pieces[7], 2, far_lift.shape[0], 2
    )
    near = lift_layer(level_one, near_lift, pieces[8])
    middle = lift_layer(wide_two, mid_lift, pieces[9])
    distant = lift_layer(wide_three, far_lift, pieces[10])
    return jnp.concatenate([near, middle, distant], axis=0)


def solution(mesh):
    return jax.shard_map(
        on_device,
        mesh=mesh,
        in_specs=(
            P(None, None, ("slab", "row", "col")),
            P(("slab", "row", "col")),
            P(("slab", "row", "col")),
            P(("slab", "row", "col")),
            P(),
            P(),
            P(),
            P(),
            P(),
            P(),
            P(),
            P(),
            P(),
            P(),
            P(),
            P(),
        ),
        out_specs=P(None, ("slab", "row"), "col"),
        check_vma=False,
    )
```

```python
import functools

import jax
import jax.numpy as jnp
from jax import lax
from jax.experimental import pallas as pl
from jax.experimental.pallas import tpu as pltpu
from jax.sharding import PartitionSpec as P

ROWS_DEV = 16
COLS_DEV = 256
PACK = 4
HALF = 16
LANES = 4
SIDE = 16
TILE = 128


def prepare_kernel(embed_ref, mix_ref, bias_ref, w1_ref, w2_ref, b1_ref, b2_ref):
    mid, feat = embed_ref.shape
    chan = mix_ref.shape[0]
    wide = w1_ref.shape[2]
    lane = lax.broadcasted_iota(jnp.int32, (feat, wide), 1)
    spread = lane // HALF == lax.broadcasted_iota(jnp.int32, (feat, wide), 0)
    spread = jnp.where(spread, 1.0, 0.0).astype(jnp.bfloat16)
    full = jnp.dot(embed_ref[...], spread, preferred_element_type=jnp.float32)
    point = lax.broadcasted_iota(jnp.int32, (mid, wide), 1) % HALF
    for q in range(HALF // PACK):
        for p in range(PACK):
            part = jnp.where(point == q * PACK + p, full, 0.0)
            w1_ref[q, p * mid : (p + 1) * mid, :] = part.astype(jnp.bfloat16)
    w2_ref[...] = jnp.zeros_like(w2_ref)
    for p in range(PACK):
        w2_ref[p * chan : (p + 1) * chan, p * mid : (p + 1) * mid] = mix_ref[...]
    both = mid + chan
    column = jnp.broadcast_to(bias_ref[:, 0:both], (both, both)).T[:, 0:1]
    for p in range(PACK):
        b1_ref[p * mid : (p + 1) * mid, :] = column[0:mid]
    b2_ref[...] = column[mid:both]


def encode_kernel(
    x_ref, count_ref, cell_ref, w1_ref, w2_ref, b1_ref, b2_ref, out_ref, place_ref,
    send_ref, ssem, rsem, place_ssem, place_rsem
):
    feat, points, _ = x_ref.shape
    tiles, _, cap = count_ref.shape
    chan = b2_ref.shape[0]
    half = tiles // 2
    col_count = lax.axis_size("col")
    me = lax.axis_index("row") * col_count + lax.axis_index("col")

    def device_of(tile):
        return {"row": tile // col_count, "col": tile % col_count}

    def encode(tile, dest_ref):
        count = count_ref[tile]
        start = pl.multiple_of(tile * cap, cap)
        best = jnp.full((chan, cap), -jnp.inf, jnp.float32)
        for h in range(points // HALF):
            block = x_ref[:, h * HALF : (h + 1) * HALF, pl.ds(start, cap)]
            block = block.reshape(feat * HALF, cap)
            for q in range(HALF // PACK):
                hidden = jnp.dot(w1_ref[q], block, preferred_element_type=jnp.float32)
                hidden = jnp.maximum(hidden + b1_ref[...], 0.0).astype(jnp.bfloat16)
                second = jnp.dot(w2_ref[...], hidden, preferred_element_type=jnp.float32)
                for p in range(PACK):
                    j = h * HALF + q * PACK + p
                    part = second[p * chan : (p + 1) * chan]
                    best = jnp.maximum(best, jnp.where(count > j, part, -jnp.inf))
        vec = jnp.maximum(best + b2_ref[...], 0.0)
        dest_ref[tile] = vec.astype(jnp.bfloat16)

    def place_of(i, slot):
        tile = (me + i) % tiles
        return pltpu.make_async_remote_copy(
            src_ref=cell_ref.at[tile],
            dst_ref=place_ref.at[slot],
            send_sem=place_ssem.at[i],
            recv_sem=place_rsem.at[i],
            device_id=device_of(tile),
            device_id_type=pl.DeviceIdType.MESH,
        )

    def copy_of(i, slot):
        tile = (me + i) % tiles
        return pltpu.make_async_remote_copy(
            src_ref=send_ref.at[tile],
            dst_ref=out_ref.at[slot],
            send_sem=ssem.at[i],
            recv_sem=rsem.at[i],
            device_id=device_of(tile),
            device_id_type=pl.DeviceIdType.MESH,
        )

    barrier = pltpu.get_barrier_semaphore()

    def greet(i, carry):
        pl.semaphore_signal(
            barrier,
            inc=1,
            device_id=device_of((me + i) % tiles),
            device_id_type=pl.DeviceIdType.MESH,
        )
        return carry

    lax.fori_loop(1, tiles, greet, 0)
    pl.semaphore_wait(barrier, tiles - 1)

    def step(k, carry):
        i = half + (1 - 2 * (k % 2)) * ((k + 1) // 2)
        encode((me + i) % tiles, send_ref)
        copy_of(i, me).start()
        place_of(i, me).start()
        return carry

    lax.fori_loop(0, tiles - 1, step, 0)
    encode(me, out_ref)
    place_ref[me] = cell_ref[me]

    def finish(i, carry):
        copy_of(i, me).wait_send()
        place_of(i, me).wait_send()
        copy_of(i, (me - i + tiles) % tiles).wait_recv()
        place_of(i, (me - i + tiles) % tiles).wait_recv()
        return carry

    lax.fori_loop(1, tiles, finish, 0)


def encode_all(points, counts, cells, embed, mix, bias):
    feat = points.shape[0]
    tiles, _, cap = counts.shape
    mid, chan = embed.shape[0], mix.shape[0]
    vmem = pl.BlockSpec(memory_space=pltpu.VMEM)
    weights = pl.pallas_call(
        prepare_kernel,
        in_specs=[vmem] * 3,
        out_specs=[vmem] * 4,
        out_shape=[
            jax.ShapeDtypeStruct((HALF // PACK, PACK * mid, feat * HALF), jnp.bfloat16),
            jax.ShapeDtypeStruct((PACK * chan, PACK * mid), jnp.bfloat16),
            jax.ShapeDtypeStruct((PACK * mid, 1), jnp.float32),
            jax.ShapeDtypeStruct((chan, 1), jnp.float32),
        ],
        name="prepare",
    )(embed, mix, bias)
    return pl.pallas_call(
        encode_kernel,
        in_specs=[vmem] * 7,
        out_specs=[vmem, vmem],
        out_shape=[
            jax.ShapeDtypeStruct((tiles, chan, cap), jnp.bfloat16),
            jax.ShapeDtypeStruct((tiles, 1, cap), jnp.int32),
        ],
        scratch_shapes=[
            pltpu.VMEM((tiles, chan, cap), jnp.bfloat16),
            pltpu.SemaphoreType.DMA((tiles,)),
            pltpu.SemaphoreType.DMA((tiles,)),
            pltpu.SemaphoreType.DMA((tiles,)),
            pltpu.SemaphoreType.DMA((tiles,)),
        ],
        compiler_params=pltpu.CompilerParams(collective_id=7, has_side_effects=True),
        name="encode_send",
    )(points, counts, cells, *weights)


def scatter_kernel(cell_ref, vec_ref, out_ref, stage, *grids):
    tiles, _, cap = vec_ref.shape
    chan = out_ref.shape[1]
    for grid in grids:
        grid[...] = jnp.zeros_like(grid)

    def per_tile(t, carry):
        stage[...] = vec_ref[t, 0:chan, :].astype(jnp.float32).T
        unroll = 8

        def per_slot(s, inner):
            for k in range(unroll):
                cells = [cell_ref[t * cap + (s * unroll + k) * LANES + a] for a in range(LANES)]
                base = (s * unroll + k) * LANES
                olds = [grids[a][pl.ds(cells[a], 1), :] for a in range(LANES)]
                for a in range(LANES):
                    grids[a][pl.ds(cells[a], 1), :] = jnp.maximum(
                        olds[a], stage[pl.ds(base + a, 1), :]
                    )
            return inner

        return lax.fori_loop(0, cap // (LANES * unroll), per_slot, carry)

    lax.fori_loop(0, tiles, per_tile, 0)
    total = grids[0][...]
    for grid in grids[1:]:
        total = jnp.maximum(total, grid[...])
    out_ref[...] = total.astype(jnp.bfloat16)


def scatter_max(cells, vectors, chan):
    tiles, _, cap = vectors.shape
    area = ROWS_DEV * COLS_DEV
    return pl.pallas_call(
        scatter_kernel,
        in_specs=[
            pl.BlockSpec(memory_space=pltpu.SMEM),
            pl.BlockSpec(memory_space=pltpu.VMEM),
        ],
        out_specs=pl.BlockSpec(memory_space=pltpu.VMEM),
        out_shape=jax.ShapeDtypeStruct((area, chan), jnp.bfloat16),
        scratch_shapes=[pltpu.VMEM((cap, chan), jnp.float32)]
        + [pltpu.VMEM((area, chan), jnp.float32)] * LANES,
        name="scatter_max",
    )(cells, vectors)


def around(count_rows, count_cols):
    return [
        (dr, dc)
        for dr in (-1, 0, 1)
        for dc in (-1, 0, 1)
        if (dr, dc) != (0, 0) and (dr == 0 or count_rows > 1) and (dc == 0 or count_cols > 1)
    ]


def span_of(step, before, size, after):
    if step > 0:
        return slice(size - before, size), slice(0, before)
    if step < 0:
        return slice(0, after), slice(before + size, before + size + after)
    return slice(0, size), slice(before, before + size)


def halo_kernel(before, after, x_ref, ext_ref, send_sem, recv_sem, *packs):
    rows, cols, chan = x_ref.shape
    part = cols // 2
    packed = {}
    if packs:
        packed = {(1, 0): packs[0:2], (-1, 0): packs[2:4]}
        for (dr, dc), (source, _) in packed.items():
            row_from = span_of(dr, before, rows, after)[0]
            source[:, :, 0:chan] = x_ref[row_from, 0:part, :]
            source[:, :, chan : 2 * chan] = x_ref[row_from, part:cols, :]
    count_rows, count_cols = lax.axis_size("row"), lax.axis_size("col")
    my_row, my_col = lax.axis_index("row"), lax.axis_index("col")
    steps = around(count_rows, count_cols)

    def exists(dr, dc):
        row, col = my_row + dr, my_col + dc
        return (row >= 0) & (row < count_rows) & (col >= 0) & (col < count_cols)

    barrier = pltpu.get_barrier_semaphore()
    for dr, dc in steps:

        @pl.when(exists(dr, dc))
        def _():
            pl.semaphore_signal(
                barrier,
                inc=1,
                device_id={"row": my_row + dr, "col": my_col + dc},
                device_id_type=pl.DeviceIdType.MESH,
            )

    peers = sum(jnp.where(exists(dr, dc), 1, 0) for dr, dc in steps)
    pl.semaphore_wait(barrier, peers)

    def copy_of(place):
        dr, dc = steps[place]
        row_from, row_to = span_of(dr, before, rows, after)
        col_from, col_to = span_of(dc, SIDE, cols, SIDE)
        source, target = x_ref.at[row_from, col_from, :], ext_ref.at[row_to, col_to, :]
        if (dr, dc) in packed:
            source, target = packed[(dr, dc)]
        return pltpu.make_async_remote_copy(
            src_ref=source,
            dst_ref=target,
            send_sem=send_sem.at[place],
            recv_sem=recv_sem.at[place],
            device_id={"row": my_row + dr, "col": my_col + dc},
            device_id_type=pl.DeviceIdType.MESH,
        )

    for place, (dr, dc) in enumerate(steps):

        @pl.when(exists(dr, dc))
        def _():
            copy_of(place).start()

    ext_ref[before : before + rows, SIDE : SIDE + cols, :] = x_ref[...]
    for dr in (-1, 0, 1):
        for dc in (-1, 0, 1):
            if (dr, dc) == (0, 0):
                continue
            row_to = span_of(dr, before, rows, after)[1]
            col_to = span_of(dc, SIDE, cols, SIDE)[1]
            shape = (row_to.stop - row_to.start, col_to.stop - col_to.start, chan)

            @pl.when(jnp.logical_not(exists(-dr, -dc)))
            def _():
                ext_ref[row_to, col_to, :] = jnp.zeros(shape, ext_ref.dtype)

    for place, (dr, dc) in enumerate(steps):

        @pl.when(exists(dr, dc))
        def _():
            copy_of(place).wait_send()

        @pl.when(exists(-dr, -dc))
        def _():
            copy_of(place).wait_recv()
            if (dr, dc) in packed:
                target = packed[(dr, dc)][1]
                row_to = span_of(dr, before, rows, after)[1]
                ext_ref[row_to, SIDE : SIDE + part, :] = target[:, :, 0:chan]
                ext_ref[row_to, SIDE + part : SIDE + cols, :] = target[:, :, chan : 2 * chan]


def with_halo(block, before, after, call_id):
    rows, cols, chan = block.shape
    count = len(around(lax.axis_size("row"), lax.axis_size("col")))
    packs = []
    if 2 * chan == TILE and lax.axis_size("row") > 1:
        for depth in (before, before, after, after):
            packs.append(pltpu.VMEM((depth, cols // 2, TILE), block.dtype))
    return pl.pallas_call(
        functools.partial(halo_kernel, before, after),
        in_specs=[pl.BlockSpec(memory_space=pltpu.VMEM)],
        out_specs=pl.BlockSpec(memory_space=pltpu.VMEM),
        out_shape=jax.ShapeDtypeStruct(
            (rows + before + after, cols + 2 * SIDE, chan), block.dtype
        ),
        scratch_shapes=[
            pltpu.SemaphoreType.DMA((count,)),
            pltpu.SemaphoreType.DMA((count,)),
        ]
        + packs,
        compiler_params=pltpu.CompilerParams(collective_id=call_id, has_side_effects=True),
        name=f"halo_{call_id}",
    )(block)


def level_kernel(
    stride, factor, bias_at, ext_ref, wa_ref, wb_ref, bias_ref, out_ref, wide_ref,
    ta, tb, stage_a, cat_a, stage_b, cat_b, wide
):
    ext_rows, ext_cols, chan_in = ext_ref.shape
    rows, cols, chan = out_ref.shape
    mid_rows, mid_cols, _ = cat_b.shape
    edge = SIDE // stride
    for w_ref, t_ref in ((wa_ref, ta), (wb_ref, tb)):
        deep = w_ref.shape[3]
        for u in range(3):
            for v in range(3):
                flip = w_ref[u, v].astype(jnp.float32).T
                t_ref[u, v * deep : (v + 1) * deep, :] = flip.astype(jnp.bfloat16)
    for stage in (stage_a, stage_b):
        stage[0:8, :] = jnp.zeros((8, stage.shape[1]), jnp.float32)
        stage[stage.shape[0] - 8 :, :] = jnp.zeros((8, stage.shape[1]), jnp.float32)

    wide[...] = jnp.zeros_like(wide)

    def gather(stage, values, count, step):
        stage[8 : 8 + values.shape[0], :] = values
        if step == 1:
            parts = [stage[7 + v : 7 + v + count, :] for v in range(3)]
        else:
            parts = [stage[pl.ds(7 + v, count, stride=step), :] for v in range(3)]
        return jnp.concatenate(parts, axis=1).astype(jnp.bfloat16)

    def first(r, carry):
        cat_a[r] = gather(stage_a, ext_ref[r].astype(jnp.float32), mid_cols, stride)
        return carry

    lax.fori_loop(0, ext_rows, first, 0, unroll=2)

    col = lax.broadcasted_iota(jnp.int32, (mid_cols, chan), 0) - edge
    col = col + lax.axis_index("col") * cols
    col_good = (col >= 0) & (col < cols * lax.axis_size("col"))
    row_base = lax.axis_index("row") * rows
    row_limit = rows * lax.axis_size("row")

    def second(i, carry):
        total = jnp.broadcast_to(bias_ref[:, bias_at : bias_at + chan], (mid_cols, chan))
        for u in range(3):
            total = total + jnp.dot(
                cat_a[stride * i + u], ta[u], preferred_element_type=jnp.float32
            )
        total = jnp.maximum(total, 0.0).astype(jnp.bfloat16).astype(jnp.float32)
        row = row_base + i - 1
        total = jnp.where(col_good & (row >= 0) & (row < row_limit), total, 0.0)
        cat_b[i] = gather(stage_b, total, mid_cols, 1)
        return carry

    lax.fori_loop(0, mid_rows, second, 0, unroll=2)

    def third(i, carry):
        total = jnp.broadcast_to(
            bias_ref[:, bias_at + chan : bias_at + 2 * chan], (mid_cols, chan)
        )
        for u in range(3):
            total = total + jnp.dot(cat_b[i + u], tb[u], preferred_element_type=jnp.float32)
        total = jnp.maximum(total, 0.0)
        total = total[edge : edge + cols]
        out_ref[i] = total.astype(jnp.bfloat16)
        if factor > 1:
            parts = chan // TILE
            for b in range(factor):
                for k in range(parts):
                    piece = total[:, k * TILE : (k + 1) * TILE]
                    wide[b * parts + k, pl.ds(b, cols, stride=factor), :] = piece
            for k in range(factor * parts):
                wide_ref[i, :, k * TILE : (k + 1) * TILE] = wide[k].astype(jnp.bfloat16)
        return carry

    lax.fori_loop(0, rows, third, 0, unroll=2)


def level(block, kernel_a, kernel_b, bias, bias_at, stride, factor, call_id):
    rows, cols, chan_in = block.shape
    before, after = (2, 2) if stride == 1 else (3, 2)
    ext = with_halo(block, before, after, call_id)
    chan = kernel_a.shape[2]
    rows_out, cols_out = rows // stride, cols // stride
    mid_rows, mid_cols = rows_out + 2, ext.shape[1] // stride
    vmem = pl.BlockSpec(memory_space=pltpu.VMEM)
    wide_shape = (rows_out, cols_out * factor, chan * factor) if factor > 1 else (1, 16, 128)
    return pl.pallas_call(
        functools.partial(level_kernel, stride, factor, bias_at),
        in_specs=[vmem] * 4,
        out_specs=[vmem, vmem],
        out_shape=[
            jax.ShapeDtypeStruct((rows_out, cols_out, chan), jnp.bfloat16),
            jax.ShapeDtypeStruct(wide_shape, jnp.bfloat16),
        ],
        scratch_shapes=[
            pltpu.VMEM((3, 3 * chan_in, chan), jnp.bfloat16),
            pltpu.VMEM((3, 3 * chan, chan), jnp.bfloat16),
            pltpu.VMEM((ext.shape[1] + 16, chan_in), jnp.float32),
            pltpu.VMEM((ext.shape[0], mid_cols, 3 * chan_in), jnp.bfloat16),
            pltpu.VMEM((mid_cols + 16, chan), jnp.float32),
            pltpu.VMEM((mid_rows, mid_cols, 3 * chan), jnp.bfloat16),
            pltpu.VMEM((factor * chan // TILE, cols_out * factor, TILE) if factor > 1 else (1, 8, TILE), jnp.float32),
        ],
        name=f"level_{call_id}",
    )(ext, kernel_a, kernel_b, bias)


def lift_layer(wide, kernel, bias_vec):
    factor = kernel.shape[0]
    rows, cols, depth = wide.shape
    weight = jnp.transpose(kernel, (2, 0, 1, 3)).reshape(kernel.shape[2], factor, depth)
    product = jnp.einsum("oak,ijk->oiaj", weight, wide, preferred_element_type=jnp.float32)
    product = product.reshape(kernel.shape[2], rows * factor, cols)
    return jax.nn.relu(product + bias_vec[:, None, None]).astype(jnp.bfloat16)


def on_device(
    points,
    pillar_cell,
    point_count,
    tile_count,
    point_embed,
    point_mix,
    first_conv,
    second_conv,
    third_conv,
    fourth_conv,
    fifth_conv,
    sixth_conv,
    near_lift,
    mid_lift,
    far_lift,
    biases,
):
    extents = [
        point_embed.shape[0],
        point_mix.shape[0],
        first_conv.shape[2],
        second_conv.shape[2],
        third_conv.shape[2],
        fourth_conv.shape[2],
        fifth_conv.shape[2],
        sixth_conv.shape[2],
        near_lift.shape[2],
        mid_lift.shape[2],
        far_lift.shape[2],
    ]
    pieces = []
    offset = 0
    for extent in extents:
        pieces.append(biases[offset : offset + extent])
        offset += extent
    tile_num = tile_count.shape[0]
    capacity = points.shape[2] // tile_num
    ncols_all = COLS_DEV * lax.axis_size("col")
    live_slot = lax.broadcasted_iota(jnp.int32, (tile_num, capacity), 1) < tile_count[:, None]
    live_points = jnp.where(live_slot, point_count.reshape(tile_num, capacity), 0)
    row_local = pillar_cell // ncols_all % ROWS_DEV
    local_cell = row_local * COLS_DEV + pillar_cell % COLS_DEV
    lead = biases.reshape(1, -1)
    vectors, places = encode_all(
        points,
        live_points.reshape(tile_num, 1, capacity),
        local_cell.reshape(tile_num, 1, capacity),
        point_embed,
        point_mix,
        lead,
    )
    chan = point_mix.shape[0]
    cells = places.reshape(-1)
    bev = scatter_max(cells, vectors, chan).reshape(ROWS_DEV, COLS_DEV, chan)
    level_one, _ = level(bev, first_conv, second_conv, lead, sum(extents[:2]), 1, 1, 0)
    level_two, wide_two = level(
        level_one, third_conv, fourth_conv, lead, sum(extents[:4]), 2, mid_lift.shape[0], 1
    )
    _, wide_three = level(
        level_two, fifth_conv, sixth_conv, lead, sum(extents[:6]), 2, far_lift.shape[0], 2
    )
    near = lift_layer(level_one, near_lift, pieces[8])
    middle = lift_layer(wide_two, mid_lift, pieces[9])
    distant = lift_layer(wide_three, far_lift, pieces[10])
    return jnp.concatenate([near, middle, distant], axis=0)


def solution(mesh):
    return jax.shard_map(
        on_device,
        mesh=mesh,
        in_specs=(
            P(None, None, ("slab", "row", "col")),
            P(("slab", "row", "col")),
            P(("slab", "row", "col")),
            P(("slab", "row", "col")),
            P(),
            P(),
            P(),
            P(),
            P(),
            P(),
            P(),
            P(),
            P(),
            P(),
            P(),
            P(),
        ),
        out_specs=P(None, ("slab", "row"), "col"),
        check_vma=False,
    )
```
